32 devices in a mesh: clients: 16 (over z, y, core), fsdp: 2 (over x).
Axes of the slice: x: 2, y: 2, z: 4, core: 2. Of those that a mesh axis runs over, the one named last changes fastest.
Arguments:
- token_ids: int32 [16, 1280], P('clients', 'fsdp'), may hold values from 0 to 16383
- target: bfloat16 [16, 1280, 768], P('clients', 'fsdp'), may hold values from -6 to 6
- embedding: bfloat16 [16384, 768], P(None, 'fsdp'), may hold values from -6 to 6
- norm_gain: float32 [768], replicated, may hold values from 0.1 to 1.9
- global_model: float32 [3, 768, 1024], P(None, 'fsdp', 'clients'), may hold values from -0.21875 to 0.21875
- global_control: float32 [3, 768, 1024], P(None, 'fsdp', 'clients'), may hold values from -140 to 140
- client_control: float32 [16, 3, 768, 1024], P('clients', None, 'fsdp'), may hold values from -150 to 150
- local_steps: int32 [16], replicated, may hold values from 1 to 2
- client_weight: int32 [16], replicated, may hold values from 1 to 4
Outputs:
- server_step: float32 [3, 768, 1024], P(None, 'fsdp', 'clients')
- server_control: float32 [3, 768, 1024], P(None, 'fsdp', 'clients')
- client_update: float32 [16, 3, 768, 1024], P('clients', None, 'fsdp')
The draws below stay inside these ranges and needn't reach their ends.
All inputs are finite; a program needn't handle non-finite values.
Results may differ from the reference program's by a relative error of at most 0.025.
Values may be sent and summed in bfloat16 or wider, within the bound.
A program may use at most 128 MiB of HBM per device.

```python
import math
import jax
import jax.numpy as jnp
import numpy as np
from jax import lax

D = 768
FF = 1024
VOCAB = 16384
LOCAL = 2
TOK_DEV = 640
GROUP_TOK = 1280
CLIENTS = 16
N_FSDP = 2


def control_common(key):
    row_key, col_key, jitter_key = jax.random.split(jax.random.fold_in(key, 7001), 3)
    lowest = 0.5
    highest = 2.0
    jitter = jax.random.truncated_normal(jitter_key, -4.0, 4.0, (3, D, FF), jnp.float32)
    row_scale = jnp.exp(jax.random.uniform(row_key, (1, D, 1), jnp.float32, math.log(lowest), math.log(highest)))
    col_scale = jnp.exp(jax.random.uniform(col_key, (1, 1, FF), jnp.float32, math.log(lowest), math.log(highest)))
    return 5.0 * row_scale * col_scale * jitter


def draw_global_control(key, part):
    return control_common(key)


def draw_client_control(key, part):
    common = control_common(key)
    drift_key, pair_key = jax.random.split(jax.random.fold_in(key, 7002), 2)
    drifts = 0.5 * jax.random.truncated_normal(drift_key, -4.0, 4.0, (CLIENTS, 3, D, FF), jnp.float32)
    pairing = jax.random.permutation(pair_key, CLIENTS)
    span_width = FF // CLIENTS
    owners = jnp.arange(FF) // span_width
    spike_factor = jnp.where(owners[None, :] == pairing[:, None], 4.0, 1.0).astype(jnp.float32)
    return common[None] + drifts * spike_factor[:, None, None, :]


def place_ends(values, own_key, low, largest):
    longest = values.shape.index(max(values.shape))
    spots = []
    for shift in (0, 1):
        where = [jax.random.randint(jax.random.fold_in(own_key, axis), (), 0, length) for axis, length in enumerate(values.shape)]
        where[longest] = (where[longest] + shift) % values.shape[longest]
        spots.append(tuple(where))
    return values.at[spots[0]].set(low).at[spots[1]].set(largest)


def block_scale(own_key, dims, shards, least, high):
    gain, own = 1.0, jax.random.fold_in(own_key, 6)
    for position, shards_of in shards:
        heights = jnp.exp(jax.random.uniform(jax.random.fold_in(own, position), (shards_of,), jnp.float32, least / len(shards), high / len(shards)))
        gain = gain * jnp.repeat(heights, dims[position] // shards_of).reshape([-1 if axis == position else 1 for axis in range(len(dims))])
    return gain


def rank_bounds(amount, slope):
    loads = [(1 << 20) // math.isqrt(standing ** slope) + 1 for standing in range(1, amount + 1)]
    spread = 1 + sum(loads) // (1 << 30)
    return np.cumsum(np.array([max(1, weight // spread) for weight in loads]))


def ranked_ids(stream_key, dims, number_of, lean):
    grid = rank_bounds(number_of, lean)
    lot = jax.random.randint(jax.random.fold_in(stream_key, 1), dims, 0, int(grid[number_of - 1]))
    grade = jnp.searchsorted(jnp.asarray(grid, jnp.int32), lot, side="right")
    return jax.random.permutation(jax.random.fold_in(stream_key, 2), number_of)[grade].astype(jnp.int32)


def centred(rng, dims, spread, reach, cuts=(), held_as=jnp.bfloat16):
    array = spread * jax.random.normal(rng, dims, jnp.float32)
    if cuts:
        array = array * block_scale(rng, dims, cuts, -0.22, 0.18)
    return jnp.clip(array, -reach, reach).astype(held_as)


def setup_inputs(seed: int = 0) -> dict:
    arg_keys = jax.random.split(jax.random.key(seed), 10)
    token_ids = place_ends(ranked_ids(arg_keys[0], (CLIENTS, GROUP_TOK), VOCAB, 2), jax.random.fold_in(arg_keys[0], 3), 0, VOCAB - 1).astype(jnp.int32)
    target = centred(arg_keys[1], (CLIENTS, GROUP_TOK, D), 1.0, 6.0, ((0, 16), (1, 2)))
    embedding = centred(arg_keys[2], (VOCAB, D), 1.0, 6.0, ((1, 2),))
    norm_gain = jnp.clip(1.0 + 0.18 * jax.random.normal(arg_keys[3], (D,), jnp.float32), 0.1, 1.9)
    global_model = centred(arg_keys[4], (3, D, FF), D ** -0.5, 0.21875, ((1, 2), (2, 16)), jnp.float32)
    global_control = draw_global_control(jax.random.fold_in(arg_keys[9], 71), 0)
    client_control = draw_client_control(jax.random.fold_in(arg_keys[9], 71), 0)
    local_steps = place_ends(jax.random.randint(arg_keys[7], (CLIENTS,), 1, LOCAL + 1), jax.random.fold_in(arg_keys[7], 1), 1, LOCAL).astype(jnp.int32)
    client_weight = place_ends(jax.random.randint(arg_keys[8], (CLIENTS,), 1, 5), jax.random.fold_in(arg_keys[8], 1), 1, 4).astype(jnp.int32)
    return {"token_ids": token_ids, "target": target, "embedding": embedding, "norm_gain": norm_gain, "global_model": global_model, "global_control": global_control, "client_control": client_control, "local_steps": local_steps, "client_weight": client_weight}


learning_rate = 0.005
norm_eps = 1e-06

def gelu_pair(pre_act):
    return jax.vjp(lambda inputs: jax.nn.gelu(inputs, approximate=True), pre_act)

def shard_grads(normed, embedded, target, current, loss_scale):
    gate_pre = jnp.dot(normed, current[0], preferred_element_type=jnp.float32)
    up_pre = jnp.dot(normed, current[1], preferred_element_type=jnp.float32)
    gate_act, gelu_back = gelu_pair(gate_pre)
    hidden = (gate_act * up_pre).astype(jnp.bfloat16)
    projected = lax.dot_general(hidden, current[2], (((1,), (1,)), ((), ())), preferred_element_type=jnp.float32)
    out_grad = ((embedded.astype(jnp.float32) + projected - target.astype(jnp.float32)) * loss_scale).astype(jnp.bfloat16)
    grad_outer = lax.dot_general(out_grad, hidden, (((0,), (0,)), ((), ())), preferred_element_type=jnp.float32)
    hidden_grad = jnp.dot(out_grad, current[2], preferred_element_type=jnp.float32)
    gate_grad = gelu_back(hidden_grad * up_pre)[0].astype(jnp.bfloat16)
    up_grad = (hidden_grad * gate_act).astype(jnp.bfloat16)
    grad_gate = lax.dot_general(normed, gate_grad, (((0,), (0,)), ((), ())), preferred_element_type=jnp.float32)
    grad_up = lax.dot_general(normed, up_grad, (((0,), (0,)), ((), ())), preferred_element_type=jnp.float32)
    return jnp.stack([grad_gate, grad_up, grad_outer])

def client_round(inputs, embedding, norm_gain, global_model, global_control):
    ids_row, target_rows, own_control, step_count = inputs
    embedded = jnp.take(embedding, ids_row, axis=0)
    widened = embedded.astype(jnp.float32)
    inv_norm = lax.rsqrt(lax.optimization_barrier(jnp.mean(widened * widened, axis=1, keepdims=True)) + norm_eps)
    normed = (widened * inv_norm * norm_gain).astype(jnp.bfloat16)
    loss_scale = 1.0 / math.sqrt(TOK_DEV * N_FSDP)
    shard_normed = normed.reshape(N_FSDP, TOK_DEV, -1)
    shard_embedded = embedded.reshape(N_FSDP, TOK_DEV, -1)
    shard_target = target_rows.reshape(N_FSDP, TOK_DEV, -1)
    correction = global_control - own_control
    pseudo = jnp.zeros(global_model.shape, jnp.float32)
    for local_step in range(LOCAL):
        current = (global_model - learning_rate * pseudo).astype(jnp.bfloat16)

        def add_shard(running, pieces):
            term = shard_grads(pieces[0], pieces[1], pieces[2], current, loss_scale)
            rounded = lax.optimization_barrier(term.astype(jnp.bfloat16))
            return (running + rounded.astype(jnp.float32), None)
        grads, _ = lax.scan(add_shard, jnp.zeros(global_model.shape, jnp.float32), (shard_normed, shard_embedded, shard_target))
        step_mask = (local_step < step_count).astype(jnp.float32)
        pseudo = pseudo + step_mask * (grads + correction)
    update = own_control - global_control + pseudo / step_count.astype(jnp.float32)
    return (pseudo, update)

def reference(token_ids, target, embedding, norm_gain, global_model, global_control, client_control, local_steps, client_weight):

    def one_client(inputs):
        return client_round(inputs, embedding, norm_gain, global_model, global_control)
    pseudo_all, client_update = lax.map(one_client, (token_ids, target, client_control, local_steps))
    weights = client_weight.astype(jnp.float32)
    weight_total = jnp.sum(weights)
    server_step = lax.optimization_barrier(jnp.sum(weights[:, None, None, None] * pseudo_all, axis=0)) / weight_total
    server_control = lax.optimization_barrier(jnp.sum(weights[:, None, None, None] * client_update, axis=0)) / weight_total
    return (server_step, server_control, client_update)
```

```python
import math

import jax
import jax.numpy as jnp
from jax import lax
from jax.sharding import PartitionSpec as P

LOCAL = 2


learning_rate = 0.005
norm_eps = 1e-06


def gelu_pair(pre_act):
    return jax.vjp(lambda inputs: jax.nn.gelu(inputs, approximate=True), pre_act)


def contract_rows(left, right):
    return lax.dot_general(
        left, right, (((0,), (0,)), ((), ())), preferred_element_type=jnp.float32
    )


def pack_owners(array, owners):
    parts, rows, columns = array.shape
    width = columns // owners
    split = array.reshape(parts, 2, rows // 2, owners, width)
    return split.transpose(3, 0, 2, 1, 4).reshape(owners, parts, rows // 2, 2 * width)


def unpack_owner(array):
    parts, half, width = array.shape
    split = array.reshape(parts, half, 2, width // 2)
    return split.transpose(0, 2, 1, 3).reshape(parts, 2 * half, width // 2)


def body(
    token_ids,
    target,
    embedding,
    norm_gain,
    global_model,
    global_control,
    client_control,
    local_steps,
    client_weight,
):
    n_clients = lax.axis_size("clients")
    n_fsdp = lax.axis_size("fsdp")
    client_index = lax.axis_index("clients")
    fsdp_index = lax.axis_index("fsdp")
    paired = n_fsdp == 2 and n_clients % 2 == 0
    if paired:
        core = client_index % 2
        role_client = client_index - core + fsdp_index
        block = core
        swap_pairs = [
            (c * 2 + f, ((c - c % 2) + f) * 2 + c % 2) for c in range(n_clients) for f in range(2)
        ]
        core_pairs = [(c, c ^ 1) for c in range(n_clients)]
    else:
        role_client = client_index
        block = fsdp_index

    def swap_roles(array):
        if not paired:
            return array
        return lax.ppermute(array, ("clients", "fsdp"), swap_pairs)

    def gather_rows(array):
        if not paired:
            return lax.all_gather(array, "fsdp", axis=0, tiled=True)
        other = lax.ppermute(array, "clients", core_pairs)
        return jnp.concatenate(
            [jnp.where(core == 0, array, other), jnp.where(core == 0, other, array)], axis=0
        )

    def reduce_rows(term):
        if not paired:
            return lax.psum_scatter(term, "fsdp", scatter_dimension=0, tiled=True).astype(
                jnp.float32
            )
        rows = term.shape[0] // 2
        own = lax.dynamic_slice_in_dim(term, core * rows, rows, axis=0)
        sent = lax.dynamic_slice_in_dim(term, (1 - core) * rows, rows, axis=0)
        received = lax.ppermute(sent, "clients", core_pairs)
        return own.astype(jnp.float32) + received.astype(jnp.float32)

    tok_rows = target.shape[1]
    group_rows = tok_rows * n_fsdp
    loss_scale = 1.0 / math.sqrt(group_rows)
    all_ids = lax.all_gather(swap_roles(token_ids), "fsdp", axis=1, tiled=True)
    emb_columns = jnp.take(embedding, all_ids[0], axis=0)
    embedded = lax.all_to_all(emb_columns, "fsdp", split_axis=0, concat_axis=1, tiled=True)
    widened = embedded.astype(jnp.float32)
    inv_norm = lax.rsqrt(jnp.mean(widened * widened, axis=1, keepdims=True) + norm_eps)
    normed = (widened * inv_norm * norm_gain).astype(jnp.bfloat16)
    target_rows = swap_roles(target[0]).astype(jnp.float32)
    model_columns = lax.all_gather(
        global_model.astype(jnp.bfloat16), "fsdp", axis=1, tiled=True
    )
    model_full = lax.all_gather(model_columns, "clients", axis=2, tiled=True)
    control_rows = lax.all_gather(
        global_control.astype(jnp.bfloat16), "clients", axis=2, tiled=True
    ).astype(global_control.dtype)
    slots = jnp.arange(local_steps.shape[0])
    step_count = jnp.sum(jnp.where(slots == client_index, local_steps, 0))
    role_steps = jnp.sum(jnp.where(slots == role_client, local_steps, 0))
    own_weight = jnp.sum(jnp.where(slots == client_index, client_weight, 0)).astype(jnp.float32)
    weight_total = jnp.sum(client_weight).astype(jnp.float32)
    correction = control_rows - client_control[0]
    parts, rows = correction.shape[0], correction.shape[1]
    role_correction = [
        swap_roles(correction[part].astype(jnp.bfloat16)).astype(jnp.float32)
        for part in range(parts)
    ]
    role_model = lax.dynamic_slice_in_dim(model_full, block * rows, rows, axis=1).astype(
        jnp.float32
    )
    gathered = [model_full[part] for part in range(parts)]
    pseudo = [jnp.zeros_like(role_correction[part]) for part in range(parts)]
    summed = [jnp.zeros_like(role_correction[part]) for part in range(parts)]
    for local_step in range(LOCAL):
        if local_step > 0:
            gathered = [
                gather_rows(
                    (role_model[part] - learning_rate * pseudo[part]).astype(jnp.bfloat16)
                )
                for part in range(parts)
            ]
        gate_pre = jnp.dot(normed, gathered[0], preferred_element_type=jnp.float32)
        up_pre = jnp.dot(normed, gathered[1], preferred_element_type=jnp.float32)
        gate_act, gelu_back = gelu_pair(gate_pre)
        hidden = (gate_act * up_pre).astype(jnp.bfloat16)
        projected = lax.dot_general(
            hidden, gathered[2], (((1,), (1,)), ((), ())), preferred_element_type=jnp.float32
        )
        out_grad = ((widened + projected - target_rows) * loss_scale).astype(jnp.bfloat16)
        outer_term = contract_rows(out_grad, hidden).astype(jnp.bfloat16)
        hidden_grad = jnp.dot(out_grad, gathered[2], preferred_element_type=jnp.float32)
        gate_grad = gelu_back(hidden_grad * up_pre)[0].astype(jnp.bfloat16)
        up_grad = (hidden_grad * gate_act).astype(jnp.bfloat16)
        gate_term = contract_rows(normed, gate_grad).astype(jnp.bfloat16)
        up_term = contract_rows(normed, up_grad).astype(jnp.bfloat16)
        grads = [reduce_rows(term) for term in (gate_term, up_term, outer_term)]
        step_mask = (local_step < role_steps).astype(jnp.float32)
        for part in range(parts):
            pseudo[part] = pseudo[part] + step_mask * (grads[part] + role_correction[part])
            summed[part] = summed[part] + step_mask * grads[part]
    own_grads = jnp.stack(
        [swap_roles(summed[part].astype(jnp.bfloat16)).astype(jnp.float32) for part in range(parts)]
    )
    taken = jnp.sum((jnp.arange(LOCAL) < step_count).astype(jnp.float32))
    own_pseudo = own_grads + taken * correction
    update = client_control[0] - control_rows + own_pseudo / step_count.astype(jnp.float32)
    packed = jnp.concatenate(
        [
            pack_owners((own_weight * own_pseudo).astype(jnp.bfloat16), n_clients),
            pack_owners((own_weight * update).astype(jnp.bfloat16), n_clients),
        ],
        axis=1,
    )
    sums = lax.psum_scatter(packed, "clients", scatter_dimension=0, tiled=True)[0]
    sums = unpack_owner(sums).astype(jnp.float32) / weight_total
    return (sums[:parts], sums[parts:], update[None])


def solution(mesh):
    placed = (
        P("clients", "fsdp"),
        P("clients", "fsdp", None),
        P(None, "fsdp"),
        P(),
        P(None, "fsdp", "clients"),
        P(None, "fsdp", "clients"),
        P("clients", None, "fsdp", None),
        P(),
        P(),
    )
    return jax.shard_map(
        body,
        mesh=mesh,
        in_specs=placed,
        out_specs=(
            P(None, "fsdp", "clients"),
            P(None, "fsdp", "clients"),
            P("clients", None, "fsdp", None),
        ),
        check_vma=False,
    )
```
